32 devices in a mesh: groups: 2 (over y), ep: 4 (over z), tok: 4 (over x, core).
Axes of the slice: x: 2, y: 2, z: 4, core: 2. Of those that a mesh axis runs over, the one named last changes fastest.
Arguments:
- tokens: bfloat16 [128, 7168], P(('groups', 'ep', 'tok')), parts along dimension 0, may hold values from -6 to 6
- expert_ids: int32 [128, 2], P(('groups', 'ep', 'tok')), parts along dimension 0, may hold values from 0 to 3, all different within a row; in each aligned block of 4 rows (0 to 3, 4 to 7, ...) at most 3 rows name the same one
- gate_fixed: int32 [128, 2], P(('groups', 'ep', 'tok')), parts along dimension 0, may hold values from 1 to 65535
- w_gate: bfloat16 [4, 7168, 2048], P('ep', None, 'tok'), may hold values from -0.0625 to 0.0625
- w_up: bfloat16 [4, 7168, 2048], P('ep', None, 'tok'), may hold values from -0.0625 to 0.0625
- w_down: bfloat16 [4, 2048, 7168], P('ep', 'tok'), may hold values from -0.125 to 0.125
Outputs:
- layer_out: bfloat16 [128, 7168], P(('groups', 'ep', 'tok')), parts along dimension 0
The draws below stay inside these ranges and needn't reach their ends.
There are 2 independent parts, one for each index of `groups`. The reference program is written for one: setup_inputs(seed, part) draws one part's arguments, and reference() takes and returns one part's arrays. A program takes and returns all parts, laid end to end along the dimension named above; an argument that names none is the same for every part. Nothing has to cross between parts.
Inputs may be any that keep to these rules, and one draw needn't show every extreme that they name: `expert_ids`: each row names 2 different experts. Among the 4 rows of one device no expert is named more than 3 times.
All inputs are finite; a program needn't handle non-finite values.
Results may differ from the reference program's by a relative error of at most 0.014.
Values may be sent and summed in bfloat16 or wider, within the bound.
No kernel may reach another device: no remote copies, remote signals or barrier semaphores. Data moves between devices by JAX's collectives and lax.ppermute only.
A program may use at most 64 MiB of HBM per device.

```python
import math
import jax
import jax.numpy as jnp
import numpy as np
from jax import lax

D = 7168
FF = 2048
TOK_DEV = 4
EXPERTS = 4
TOPK = 2
MOST = 3
TOKENS = 64
N_TOK = 4


def touch_ends(drawn, key, smallest, top_value):
    longest = drawn.shape.index(max(drawn.shape))
    spots = []
    for shift in (0, 1):
        where = [jax.random.randint(jax.random.fold_in(key, axis), (), 0, length) for axis, length in enumerate(drawn.shape)]
        where[longest] = (where[longest] + shift) % drawn.shape[longest]
        spots.append(tuple(where))
    return drawn.at[spots[0]].set(smallest).at[spots[1]].set(top_value)


def level_of(own_key, shape, split, least, top_value):
    level, own = 1.0, jax.random.fold_in(own_key, 6)
    for axis_at, shards_of in split:
        draws = jnp.exp(jax.random.uniform(jax.random.fold_in(own, axis_at), (shards_of,), jnp.float32, least / len(split), top_value / len(split)))
        level = level * jnp.repeat(draws, shape[axis_at] // shards_of).reshape([-1 if axis == axis_at else 1 for axis in range(len(shape))])
    return level


def shared_out(own_key, own, number, rows, amount, top, most, lean):
    ranking = jax.random.permutation(own_key, amount)
    heavy_load, ordinary = load_shares(amount, rows * top, most, lean, True), load_shares(amount, rows * top, most, lean, False)
    places = jnp.arange(amount)

    def named(sizes, offset_by):
        used = int((sizes > 0).sum())
        fixed = max(1, used // 4)
        passed = fixed + (places - fixed + offset_by * (used - fixed)) % max(1, amount - fixed)
        return jnp.zeros((amount,), jnp.int32).at[ranking[jnp.where(places < fixed, places, passed)]].set(jnp.asarray(sizes, jnp.int32))

    sizes = jnp.where(number % 4 == 0, named(heavy_load, number // 4), named(ordinary, number - number // 4 - 1))
    mixed = jax.random.permutation(jax.random.fold_in(own, 3), amount)
    giver, receiver = mixed[0:amount // 2 * 2:2], mixed[1:amount // 2 * 2:2]
    room = jnp.minimum(sizes[giver] - 1, most - sizes[receiver]) // 2
    room = jnp.where((giver == ranking[0]) | (receiver == ranking[0]) | (sizes[receiver] == 0), 0, jnp.maximum(room, 0))
    passed = jax.random.randint(jax.random.fold_in(own, 4), (amount // 2,), 0, 1 << 20) % (room + 1)
    sizes = sizes.at[giver].add(-passed).at[receiver].add(passed)
    labels = jnp.searchsorted(jnp.cumsum(sizes), jnp.arange(rows * top), side="right").astype(jnp.int32)
    grid = labels.reshape(top, rows).T
    grid = grid[jax.random.permutation(jax.random.fold_in(own, 1), rows)]
    offset_by = jax.random.randint(jax.random.fold_in(own, 2), (rows, 1), 0, top)
    return jnp.take_along_axis(grid, (jnp.arange(top)[None, :] + offset_by) % top, axis=1)


def load_shares(amount, total, reach, slope, full):
    weights = [(1 << 20) // math.isqrt(grade ** slope) + 1 for grade in range(1, amount + 1)]
    largest = reach if full else min(reach, max(-(-total // amount), total * weights[0] // sum(weights)))
    least = 1 if total - largest >= amount - 1 else 0
    holding, spare = [largest] + [least] * (amount - 1), total - largest - least * (amount - 1)
    while spare > 0:
        candidates = [i for i in range(1, amount) if holding[i] < largest] or [i for i in range(1, amount) if holding[i] < reach]
        whole, left = sum([weights[i] for i in candidates]), spare
        for i in candidates:
            extra = min(reach - holding[i], max(1, left * weights[i] // whole), spare)
            holding[i] = holding[i] + extra
            spare = spare - extra
    return np.array(holding)


def scatter_about(own_key, extent, spread, limit, shards=(), kind=jnp.bfloat16):
    result = spread * jax.random.normal(own_key, extent, jnp.float32)
    if shards:
        result = result * level_of(own_key, extent, shards, -0.22, 0.18)
    return jnp.clip(result, -limit, limit).astype(kind)


def setup_inputs(seed: int = 0, part: int = 0) -> dict:
    seeds = jax.random.split(jax.random.key(seed), 7)
    part_splits = jax.random.split(jax.random.fold_in(seeds[6], part), 7)
    tokens = scatter_about(part_splits[0], (TOKENS, D), 1.0, 6.0, ((0, 16),))
    expert_ids_keys = jax.random.split(jax.random.fold_in(part_splits[1], 1), TOKENS // TOK_DEV)
    expert_ids_turns = jax.random.permutation(jax.random.fold_in(part_splits[1], 3), TOKENS // TOK_DEV)
    expert_ids = jax.vmap(lambda own, number: shared_out(jax.random.fold_in(part_splits[1], 2), own, number, TOK_DEV, EXPERTS, TOPK, MOST, 2))(expert_ids_keys, expert_ids_turns).reshape((TOKENS, TOPK))
    gate_fixed = touch_ends(jax.random.randint(part_splits[2], (TOKENS, TOPK), 1, 65536), jax.random.fold_in(part_splits[2], 1), 1, 65535).astype(jnp.int32)
    w_gate = scatter_about(seeds[3], (EXPERTS, D, FF), D ** -0.5, 0.0625, ((0, 4), (2, 4)))
    w_up = scatter_about(seeds[4], (EXPERTS, D, FF), D ** -0.5, 0.0625, ((0, 4), (2, 4)))
    w_down = scatter_about(seeds[5], (EXPERTS, FF, D), FF ** -0.5, 0.125, ((0, 4), (1, 4)))
    return dict(tokens=tokens, expert_ids=expert_ids, gate_fixed=gate_fixed, w_gate=w_gate, w_up=w_up, w_down=w_down)


def reference(tokens, expert_ids, gate_fixed, w_gate, w_up, w_down):
    scores = gate_fixed.astype(jnp.float32)
    weights = 2.5 * scores / jnp.sum(scores, axis=1, keepdims=True)
    slab_width = FF // N_TOK
    summed = jnp.zeros((TOKENS, D), jnp.float32)
    for expert in range(EXPERTS):
        gate = jnp.dot(tokens, w_gate[expert], preferred_element_type=jnp.float32)
        up_val = jnp.dot(tokens, w_up[expert], preferred_element_type=jnp.float32)
        hidden = (jax.nn.silu(gate) * up_val).astype(jnp.bfloat16)
        expert_out = jnp.zeros((TOKENS, D), jnp.float32)
        for slab in range(N_TOK):
            lower = slab * slab_width
            partial_value = jnp.dot(hidden[:, lower:lower + slab_width], w_down[expert, lower:lower + slab_width, :], preferred_element_type=jnp.float32)
            partial_value = lax.optimization_barrier(partial_value.astype(jnp.bfloat16)).astype(jnp.float32)
            expert_out = expert_out + partial_value
        weight_e = jnp.sum(weights * (expert_ids == expert).astype(jnp.float32), axis=1)
        summed = summed + weight_e[:, None] * expert_out
    return summed.astype(jnp.bfloat16)
```

```python
import functools

import jax
import jax.numpy as jnp
from jax import lax
from jax.experimental import pallas as pl
from jax.experimental.pallas import tpu as pltpu
from jax.sharding import PartitionSpec as P


CORES = 2
MIB = 1 << 20
VMEM_BYTES = 58 * MIB


def shift(value, axis, amount):
    size = lax.axis_size(axis)
    return lax.ppermute(value, axis, [(i, (i + amount) % size) for i in range(size)])


def core_swap(value):
    size = lax.axis_size("tok")
    return lax.ppermute(value, "tok", [(i, i ^ 1) for i in range(size)])


def fetch_all(pairs, semaphores):
    copies = [pltpu.make_async_copy(s, t, semaphores.at[i]) for i, (s, t) in enumerate(pairs)]
    for copy in copies:
        copy.start()
    for copy in copies:
        copy.wait()


def open_kernel(cut, gate_ref, up_ref, gate_out, up_out, semaphores):
    pairs = [(gate_ref, gate_out)]
    if cut:
        pairs.append((up_ref.at[pl.ds(0, cut)], up_out.at[pl.ds(0, cut)]))
    fetch_all(pairs, semaphores)


def rest_kernel(cut, held_ref, up_ref, up_out, semaphores):
    span = pl.ds(cut, up_ref.shape[0] - cut)
    fetch_all([(up_ref.at[span], up_out.at[span])], semaphores)


def kernel_limit(weight, extra=0):
    return VMEM_BYTES - 4 * weight.size - 6 * MIB + extra * MIB


def load_open(gate_w, up_w, cut):
    hbm = pl.BlockSpec(memory_space=pltpu.HBM)
    vmem = pl.BlockSpec(memory_space=pltpu.VMEM)
    return pl.pallas_call(
        functools.partial(open_kernel, cut),
        out_shape=[jax.ShapeDtypeStruct(w.shape, w.dtype) for w in (gate_w, up_w)],
        in_specs=[hbm, hbm],
        out_specs=[vmem, vmem],
        scratch_shapes=[pltpu.SemaphoreType.DMA((2,))],
        compiler_params=pltpu.CompilerParams(vmem_limit_bytes=kernel_limit(gate_w)),
        name="load_open",
    )(gate_w, up_w)


def load_rest(held, up_w, cut):
    hbm = pl.BlockSpec(memory_space=pltpu.HBM)
    vmem = pl.BlockSpec(memory_space=pltpu.VMEM)
    return pl.pallas_call(
        functools.partial(rest_kernel, cut),
        out_shape=jax.ShapeDtypeStruct(up_w.shape, up_w.dtype),
        in_specs=[vmem, hbm],
        out_specs=vmem,
        input_output_aliases={0: 0},
        scratch_shapes=[pltpu.SemaphoreType.DMA((2,))],
        compiler_params=pltpu.CompilerParams(vmem_limit_bytes=kernel_limit(up_w, 3)),
        name="load_rest",
    )(held, up_w)


def ffn_kernel(count, depth, width, *refs):
    chunks = refs[:count]
    gate_ref, up_ref, down_ref = refs[count:count + 3]
    outs = refs[count + 3:2 * count + 3]
    gate_sum, up_sum, hidden, down_vmem, semaphore = refs[2 * count + 3:]
    fetch = pltpu.make_async_copy(down_ref, down_vmem, semaphore)
    fetch.start()
    rows, model = chunks[0].shape
    gate_sum[...] = jnp.zeros_like(gate_sum)
    up_sum[...] = jnp.zeros_like(up_sum)

    def project(i, carry):
        span = pl.ds(pl.multiple_of(i * depth, depth), depth)
        tokens = jnp.concatenate([c[:, span].astype(jnp.float32) for c in chunks], axis=0).astype(jnp.bfloat16)
        gate_sum[...] += jnp.dot(tokens, gate_ref[span, :], preferred_element_type=jnp.float32)
        up_sum[...] += jnp.dot(tokens, up_ref[span, :], preferred_element_type=jnp.float32)
        return carry

    lax.fori_loop(0, model // depth, project, 0)
    gate = gate_sum[...]
    hidden[...] = (gate / (1.0 + jnp.exp(-gate)) * up_sum[...]).astype(jnp.bfloat16)

    fetch.wait()

    def expand(i, carry):
        span = pl.ds(pl.multiple_of(i * width, width), width)
        partial = jnp.dot(hidden[...], down_vmem[:, span], preferred_element_type=jnp.float32)
        for j, out in enumerate(outs):
            out[:, span] = partial[j * rows:(j + 1) * rows].astype(jnp.bfloat16)
        return carry

    lax.fori_loop(0, model // width, expand, 0)


def ffn(chunks, gate_w, up_w, down_w):
    count = len(chunks)
    rows, model = chunks[0].shape
    units = gate_w.shape[1]
    total = count * rows
    block = 1024 if model % 1024 == 0 else model
    vmem = pl.BlockSpec(memory_space=pltpu.VMEM)
    return pl.pallas_call(
        functools.partial(ffn_kernel, count, block, block),
        out_shape=[jax.ShapeDtypeStruct((rows, model), jnp.bfloat16)] * count,
        in_specs=[vmem] * (count + 2) + [pl.BlockSpec(memory_space=pltpu.HBM)],
        out_specs=[vmem] * count,
        scratch_shapes=[
            pltpu.VMEM((total, units), jnp.float32),
            pltpu.VMEM((total, units), jnp.float32),
            pltpu.VMEM((total, units), jnp.bfloat16),
            pltpu.VMEM(down_w.shape, down_w.dtype),
            pltpu.SemaphoreType.DMA,
        ],
        compiler_params=pltpu.CompilerParams(vmem_limit_bytes=kernel_limit(gate_w)),
        cost_estimate=pl.CostEstimate(
            flops=6 * total * model * units,
            bytes_accessed=6 * model * units + 4 * total * model,
            transcendentals=total * units,
        ),
        name="ffn",
    )(*chunks, gate_w, up_w, down_w)


def combine_kernel(ids_ref, gate_ref, *refs):
    terms, out = refs[:-1], refs[-1]
    me = lax.axis_index("ep")
    ids = ids_ref[...]
    scores = gate_ref[...].astype(jnp.float32)
    weights = 2.5 * scores / jnp.sum(scores, axis=1, keepdims=True)
    total = jnp.zeros(out.shape, jnp.float32)
    for k, term in enumerate(terms):
        label = lax.rem(me + k, len(terms))
        weight = jnp.sum(jnp.where(ids == label, weights, 0.0), axis=1, keepdims=True)
        total = total + weight * term[...].astype(jnp.float32)
    out[...] = total.astype(jnp.bfloat16)


def combine(expert_ids, gate_fixed, terms):
    vmem = pl.BlockSpec(memory_space=pltpu.VMEM)
    return pl.pallas_call(
        combine_kernel,
        out_shape=jax.ShapeDtypeStruct(terms[0].shape, jnp.bfloat16),
        in_specs=[vmem] * (len(terms) + 2),
        out_specs=vmem,
        compiler_params=pltpu.CompilerParams(vmem_limit_bytes=8 * MIB),
        name="combine",
    )(expert_ids, gate_fixed, *terms)


def per_device(tokens, expert_ids, gate_fixed, w_gate, w_up, w_down):
    n_ep = lax.axis_size("ep")
    n_x = lax.axis_size("tok") // CORES
    columns = [tokens]
    for k in range(1, n_ep):
        columns.append(shift(tokens, "ep", k))
    planes = []
    for k in range(n_ep):
        for j in range(n_x):
            planes.append(columns[k] if j == 0 else shift(columns[k], "tok", CORES * j))
    mirrored = []
    for n, chunk in enumerate(planes):
        mirrored.append(core_swap(chunk))
    gate_w, held = load_open(w_gate[0], w_up[0], w_up.shape[1] // 4)
    up_w = load_rest(held, w_up[0], w_up.shape[1] // 4)
    parts = ffn(planes + mirrored, gate_w, up_w, w_down[0])
    half = len(planes)
    terms = []
    for k in range(n_ep):
        total = None
        for j in range(n_x):
            n = k * n_x + j
            other = core_swap(parts[half + n])
            both = parts[n].astype(jnp.float32) + other.astype(jnp.float32)
            if j:
                both = shift(both.astype(jnp.bfloat16), "tok", -CORES * j).astype(jnp.float32)
            total = both if total is None else total + both
        total = total.astype(jnp.bfloat16)
        if k:
            total = shift(total, "ep", -k)
        terms.append(total)
    return combine(expert_ids, gate_fixed, terms)


def solution(mesh):
    in_specs = (
        P(("groups", "ep", "tok"), None),
        P(("groups", "ep", "tok"), None),
        P(("groups", "ep", "tok"), None),
        P("ep", None, "tok"),
        P("ep", None, "tok"),
        P("ep", "tok", None),
    )
    out_specs = P(("groups", "ep", "tok"), None)
    return jax.shard_map(
        per_device, mesh=mesh, in_specs=in_specs, out_specs=out_specs, check_vma=False
    )
```

```python
import functools

import jax
import jax.numpy as jnp
from jax import lax
from jax.experimental import pallas as pl
from jax.experimental.pallas import tpu as pltpu
from jax.sharding import PartitionSpec as P


CORES = 2
MIB = 1 << 20
VMEM_BYTES = 62 * MIB


def shift(value, axis, amount):
    size = lax.axis_size(axis)
    return lax.ppermute(value, axis, [(i, (i + amount) % size) for i in range(size)])


def core_swap(value):
    size = lax.axis_size("tok")
    return lax.ppermute(value, "tok", [(i, i ^ 1) for i in range(size)])


def enter_kernel(gate_ref, up_ref, out_ref):
    out_ref[...] = jnp.zeros_like(out_ref)


def enter(gate_w, up_w):
    hbm = pl.BlockSpec(memory_space=pl.ANY)
    return pl.pallas_call(
        enter_kernel,
        out_shape=jax.ShapeDtypeStruct((8, 128), jnp.float32),
        in_specs=[hbm, hbm],
        out_specs=pl.BlockSpec(memory_space=pltpu.VMEM),
        compiler_params=pltpu.CompilerParams(vmem_limit_bytes=VMEM_BYTES - 4 * gate_w.size - int(0.75 * MIB)),
        name="enter",
    )(gate_w, up_w)


def kernel_limit(weight, extra=0):
    return VMEM_BYTES - 4 * weight.size - 15 * MIB + extra * MIB


def ffn_kernel(count, depth, width, *refs):
    chunks = refs[:count]
    gate_ref, up_ref, down_ref, _ = refs[count:count + 4]
    outs = refs[count + 4:2 * count + 4]
    gate_sum, up_sum, hidden, down_vmem, semaphore = refs[2 * count + 4:]
    fetch = pltpu.make_async_copy(down_ref, down_vmem, semaphore)
    fetch.start()
    rows, model = chunks[0].shape
    gate_sum[...] = jnp.zeros_like(gate_sum)
    up_sum[...] = jnp.zeros_like(up_sum)

    def project(i, carry):
        span = pl.ds(pl.multiple_of(i * depth, depth), depth)
        tokens = jnp.concatenate([c[:, span].astype(jnp.float32) for c in chunks], axis=0).astype(jnp.bfloat16)
        gate_sum[...] += jnp.dot(tokens, gate_ref[span, :], preferred_element_type=jnp.float32)
        up_sum[...] += jnp.dot(tokens, up_ref[span, :], preferred_element_type=jnp.float32)
        return carry

    lax.fori_loop(0, model // depth, project, 0)
    gate = gate_sum[...]
    hidden[...] = (gate / (1.0 + jnp.exp(-gate)) * up_sum[...]).astype(jnp.bfloat16)

    fetch.wait()

    def expand(i, carry):
        span = pl.ds(pl.multiple_of(i * width, width), width)
        partial = jnp.dot(hidden[...], down_vmem[:, span], preferred_element_type=jnp.float32)
        for j, out in enumerate(outs):
            out[:, span] = partial[j * rows:(j + 1) * rows].astype(jnp.bfloat16)
        return carry

    lax.fori_loop(0, model // width, expand, 0)


def ffn(chunks, gate_w, up_w, down_w, entered):
    count = len(chunks)
    rows, model = chunks[0].shape
    units = gate_w.shape[1]
    total = count * rows
    block = 1024 if model % 1024 == 0 else model
    vmem = pl.BlockSpec(memory_space=pltpu.VMEM)
    return pl.pallas_call(
        functools.partial(ffn_kernel, count, block, block),
        out_shape=[jax.ShapeDtypeStruct((rows, model), jnp.bfloat16)] * count,
        in_specs=[vmem] * (count + 2) + [pl.BlockSpec(memory_space=pl.ANY)] * 2,
        out_specs=[vmem] * count,
        scratch_shapes=[
            pltpu.VMEM((total, units), jnp.float32),
            pltpu.VMEM((total, units), jnp.float32),
            pltpu.VMEM((total, units), jnp.bfloat16),
            pltpu.VMEM(down_w.shape, down_w.dtype),
            pltpu.SemaphoreType.DMA,
        ],
        compiler_params=pltpu.CompilerParams(vmem_limit_bytes=kernel_limit(gate_w)),
        cost_estimate=pl.CostEstimate(
            flops=6 * total * model * units,
            bytes_accessed=6 * model * units + 4 * total * model,
            transcendentals=total * units,
        ),
        name="ffn",
    )(*chunks, gate_w, up_w, down_w, entered)


def combine_kernel(ids_ref, gate_ref, *refs):
    terms, out = refs[:-1], refs[-1]
    me = lax.axis_index("ep")
    ids = ids_ref[...]
    scores = gate_ref[...].astype(jnp.float32)
    weights = 2.5 * scores / jnp.sum(scores, axis=1, keepdims=True)
    total = jnp.zeros(out.shape, jnp.float32)
    for k, term in enumerate(terms):
        label = lax.rem(me + k, len(terms))
        weight = jnp.sum(jnp.where(ids == label, weights, 0.0), axis=1, keepdims=True)
        total = total + weight * term[...].astype(jnp.float32)
    out[...] = total.astype(jnp.bfloat16)


def combine(expert_ids, gate_fixed, terms):
    vmem = pl.BlockSpec(memory_space=pltpu.VMEM)
    return pl.pallas_call(
        combine_kernel,
        out_shape=jax.ShapeDtypeStruct(terms[0].shape, jnp.bfloat16),
        in_specs=[vmem] * (len(terms) + 2),
        out_specs=vmem,
        compiler_params=pltpu.CompilerParams(vmem_limit_bytes=8 * MIB),
        name="combine",
    )(expert_ids, gate_fixed, *terms)


def per_device(tokens, expert_ids, gate_fixed, w_gate, w_up, w_down):
    n_ep = lax.axis_size("ep")
    n_x = lax.axis_size("tok") // CORES
    entered = enter(w_gate[0], w_up[0])
    columns = [tokens]
    for k in range(1, n_ep):
        columns.append(shift(tokens, "ep", k))
    planes = []
    for k in range(n_ep):
        for j in range(n_x):
            planes.append(columns[k] if j == 0 else shift(columns[k], "tok", CORES * j))
    mirrored = []
    for n, chunk in enumerate(planes):
        mirrored.append(core_swap(chunk))
    parts = ffn(planes + mirrored, w_gate[0], w_up[0], w_down[0], entered)
    half = len(planes)
    terms = []
    for k in range(n_ep):
        total = None
        for j in range(n_x):
            n = k * n_x + j
            other = core_swap(parts[half + n])
            both = parts[n].astype(jnp.float32) + other.astype(jnp.float32)
            if j:
                both = shift(both.astype(jnp.bfloat16), "tok", -CORES * j).astype(jnp.float32)
            total = both if total is None else total + both
        total = total.astype(jnp.bfloat16)
        if k:
            total = shift(total, "ep", -k)
        terms.append(total)
    return combine(expert_ids, gate_fixed, terms)


def solution(mesh):
    in_specs = (
        P(("groups", "ep", "tok"), None),
        P(("groups", "ep", "tok"), None),
        P(("groups", "ep", "tok"), None),
        P("ep", None, "tok"),
        P("ep", None, "tok"),
        P("ep", "tok", None),
    )
    out_specs = P(("groups", "ep", "tok"), None)
    return jax.shard_map(
        per_device, mesh=mesh, in_specs=in_specs, out_specs=out_specs, check_vma=False
    )
```

```python
import functools

import jax
import jax.numpy as jnp
from jax import lax
from jax.experimental import pallas as pl
from jax.experimental.pallas import tpu as pltpu
from jax.sharding import PartitionSpec as P


CORES = 2
MIB = 1 << 20
VMEM_BYTES = 62 * MIB


def shift(value, axis, amount, stride=1):
    size = lax.axis_size(axis) // stride
    pairs = [(i * stride + r, (i + amount) % size * stride + r) for i in range(size) for r in range(stride)]
    return lax.ppermute(value, axis, pairs)


def core_swap(value):
    size = lax.axis_size("tok")
    return lax.ppermute(value, "tok", [(i, i ^ 1) for i in range(size)])


def enter_kernel(gate_ref, up_ref, out_ref):
    out_ref[...] = jnp.zeros_like(out_ref)


def enter(gate_w, up_w):
    hbm = pl.BlockSpec(memory_space=pl.ANY)
    return pl.pallas_call(
        enter_kernel,
        out_shape=jax.ShapeDtypeStruct((8, 128), jnp.float32),
        in_specs=[hbm, hbm],
        out_specs=pl.BlockSpec(memory_space=pltpu.VMEM),
        compiler_params=pltpu.CompilerParams(vmem_limit_bytes=VMEM_BYTES - 4 * gate_w.size - 3 * MIB // 4),
        name="enter",
    )(gate_w, up_w)


def gather_kernel(*refs):
    for i, ref in enumerate(refs[:-1]):
        refs[-1][i] = ref[...]


def gather_rows(chunks):
    rows, model = chunks[0].shape
    vmem = pl.BlockSpec(memory_space=pltpu.VMEM)
    return pl.pallas_call(
        gather_kernel,
        out_shape=jax.ShapeDtypeStruct((len(chunks), rows, model), chunks[0].dtype),
        in_specs=[vmem] * len(chunks),
        out_specs=vmem,
        compiler_params=pltpu.CompilerParams(vmem_limit_bytes=2 * MIB),
    )(*chunks)


def pieces(refs):
    return [ref.at[i] for ref in refs for i in range(ref.shape[0])]


def ffn_kernel(n_in, n_out, depth, width, *refs):
    chunks = pieces(refs[:n_in])
    gate_ref, up_ref, down_ref, _ = refs[n_in:n_in + 4]
    outs = pieces(refs[n_in + 4:n_in + 4 + n_out])
    gate_sum, up_sum, hidden, down_vmem, semaphore = refs[n_in + 4 + n_out:]
    fetch = pltpu.make_async_copy(down_ref, down_vmem, semaphore)
    fetch.start()
    rows, model = chunks[0].shape
    gate_sum[...] = jnp.zeros_like(gate_sum)
    up_sum[...] = jnp.zeros_like(up_sum)

    def project(i, carry):
        span = pl.ds(pl.multiple_of(i * depth, depth), depth)
        tokens = jnp.concatenate([c[:, span].astype(jnp.float32) for c in chunks], axis=0).astype(jnp.bfloat16)
        gate_sum[...] += jnp.dot(tokens, gate_ref[span, :], preferred_element_type=jnp.float32)
        up_sum[...] += jnp.dot(tokens, up_ref[span, :], preferred_element_type=jnp.float32)
        return carry

    lax.fori_loop(0, model // depth, project, 0)
    gate = gate_sum[...]
    hidden[...] = (gate / (1.0 + jnp.exp(-gate)) * up_sum[...]).astype(jnp.bfloat16)
    fetch.wait()

    def expand(i, carry):
        span = pl.ds(pl.multiple_of(i * width, width), width)
        partial = jnp.dot(hidden[...], down_vmem[:, span], preferred_element_type=jnp.float32)
        for j, out in enumerate(outs):
            out[:, span] = partial[j * rows:(j + 1) * rows].astype(jnp.bfloat16)
        return carry

    lax.fori_loop(0, model // width, expand, 0)


def block_of(model, most):
    return max(b for b in range(128, most + 1, 128) if model % b == 0)


def ffn(blocks, out_counts, gate_w, up_w, down_w, entered):
    _, rows, model = blocks[0].shape
    units = gate_w.shape[1]
    total = rows * sum(b.shape[0] for b in blocks)
    vmem = pl.BlockSpec(memory_space=pltpu.VMEM)
    return pl.pallas_call(
        functools.partial(ffn_kernel, len(blocks), len(out_counts), block_of(model, DEPTH), block_of(model, WIDTH)),
        out_shape=[jax.ShapeDtypeStruct((n, rows, model), jnp.bfloat16) for n in out_counts],
        in_specs=[vmem] * (len(blocks) + 2) + [pl.BlockSpec(memory_space=pl.ANY)] * 2,
        out_specs=[vmem] * len(out_counts),
        scratch_shapes=[
            pltpu.VMEM((total, units), jnp.float32),
            pltpu.VMEM((total, units), jnp.float32),
            pltpu.VMEM((total, units), jnp.bfloat16),
            pltpu.VMEM(down_w.shape, down_w.dtype),
            pltpu.SemaphoreType.DMA,
        ],
        compiler_params=pltpu.CompilerParams(vmem_limit_bytes=VMEM_BYTES - 4 * gate_w.size - 15 * MIB),
        cost_estimate=pl.CostEstimate(
            flops=6 * total * model * units,
            bytes_accessed=6 * model * units + 4 * total * model,
            transcendentals=total * units,
        ),
        name="ffn",
    )(*blocks, gate_w, up_w, down_w, entered)


DEPTH = 1792
WIDTH = 1792


def combine_kernel(ids_ref, gate_ref, *refs):
    terms, out = refs[:-1], refs[-1]
    me = lax.axis_index("ep")
    ids = ids_ref[...]
    scores = gate_ref[...].astype(jnp.float32)
    weights = 2.5 * scores / jnp.sum(scores, axis=1, keepdims=True)
    total = jnp.zeros(out.shape, jnp.float32)
    for k, term in enumerate(terms):
        label = lax.rem(me + k, len(terms))
        weight = jnp.sum(jnp.where(ids == label, weights, 0.0), axis=1, keepdims=True)
        total = total + weight * term[0].astype(jnp.float32)
    out[...] = total.astype(jnp.bfloat16)


def combine(expert_ids, gate_fixed, terms):
    vmem = pl.BlockSpec(memory_space=pltpu.VMEM)
    return pl.pallas_call(
        combine_kernel,
        out_shape=jax.ShapeDtypeStruct(terms[0].shape[1:], jnp.bfloat16),
        in_specs=[vmem] * (len(terms) + 2),
        out_specs=vmem,
        compiler_params=pltpu.CompilerParams(vmem_limit_bytes=8 * MIB),
        name="combine",
    )(expert_ids, gate_fixed, *terms)


def sum_kernel(spans, *refs):
    out = refs[-1]
    for i in range(out.shape[0]):
        total = refs[0][spans[0] + i].astype(jnp.float32)
        for ref, first in zip(refs[1:-1], spans[1:]):
            total = total + ref[first + i].astype(jnp.float32)
        out[i] = total.astype(out.dtype)


def add(count, *terms):
    vmem = pl.BlockSpec(memory_space=pltpu.VMEM)
    arrays = [array for array, _ in terms]
    rows, model = arrays[0].shape[1:]
    return pl.pallas_call(
        functools.partial(sum_kernel, [first for _, first in terms]),
        out_shape=jax.ShapeDtypeStruct((count, rows, model), arrays[0].dtype),
        in_specs=[vmem] * len(arrays),
        out_specs=vmem,
        compiler_params=pltpu.CompilerParams(vmem_limit_bytes=4 * MIB),
    )(*arrays)


def per_device(tokens, expert_ids, gate_fixed, w_gate, w_up, w_down):
    n_ep = lax.axis_size("ep")
    n_x = lax.axis_size("tok") // CORES
    entered = enter(w_gate[0], w_up[0])
    arrived = [shift(tokens, "ep", k) for k in range(1, n_ep)]
    lines = [tokens] + [shift(tokens, "tok", j, CORES) for j in range(1, n_x)]
    stacks = [gather_rows([tokens]), gather_rows(arrived)]
    for j in range(1, n_x):
        stacks += [lines[j][None], shift(stacks[1], "tok", j, CORES)]
    mirrored = [core_swap(s) for s in stacks]
    sizes = [n_ep] + [n_ep - 1, 1] * (n_x - 1)
    parts = ffn(stacks + mirrored, sizes * CORES, w_gate[0], w_up[0], w_down[0], entered)
    mine, theirs = parts[:len(sizes)], parts[len(sizes):]
    far = [[] for _ in range(n_ep)]
    spans = ((0, n_ep - 1, 1), (1, n_ep - 2, 1), (2, 0, n_ep - 2))
    for j in range(1, n_x):
        last, rest = 2 * j, 2 * j - 1
        tail = core_swap(theirs[last])
        body = core_swap(theirs[rest])
        for part, first, count in spans:
            pair = ((mine[last], 0), (tail, 0)) if part == 0 else ((mine[rest], first), (body, first))
            value = shift(add(count, *pair), "tok", -j, CORES)
            for k in range(count):
                far[first + k].append((value, k))
    near = core_swap(theirs[0])
    terms = []
    for k in range(n_ep):
        total = add(1, (mine[0], k), (near, k), *far[k])
        terms.append(shift(total, "ep", -k) if k else total)
    return combine(expert_ids, gate_fixed, terms)


def solution(mesh):
    in_specs = (
        P(("groups", "ep", "tok"), None),
        P(("groups", "ep", "tok"), None),
        P(("groups", "ep", "tok"), None),
        P("ep", None, "tok"),
        P("ep", None, "tok"),
        P("ep", "tok", None),
    )
    out_specs = P(("groups", "ep", "tok"), None)
    return jax.shard_map(
        per_device, mesh=mesh, in_specs=in_specs, out_specs=out_specs, check_vma=False
    )
```

```python
import functools

import jax
import jax.numpy as jnp
from jax import lax
from jax.experimental import pallas as pl
from jax.experimental.pallas import tpu as pltpu
from jax.sharding import PartitionSpec as P


CORES = 2
MIB = 1 << 20
VMEM_BYTES = 62 * MIB


def mirrors(size):
    return XOR and size & (size - 1) == 0


def shift(value, axis, amount, stride=1):
    size = lax.axis_size(axis) // stride
    target = (lambda i: i ^ abs(amount)) if mirrors(size) else (lambda i: (i + amount) % size)
    pairs = [(i * stride + r, target(i) * stride + r) for i in range(size) for r in range(stride)]
    return lax.ppermute(value, axis, pairs)


def core_swap(value):
    size = lax.axis_size("tok")
    return lax.ppermute(value, "tok", [(i, i ^ 1) for i in range(size)])


def enter_kernel(gate_ref, up_ref, out_ref):
    out_ref[...] = jnp.zeros_like(out_ref)


def enter(gate_w, up_w):
    hbm = pl.BlockSpec(memory_space=pl.ANY)
    return pl.pallas_call(
        enter_kernel,
        out_shape=jax.ShapeDtypeStruct((8, 128), jnp.float32),
        in_specs=[hbm, hbm],
        out_specs=pl.BlockSpec(memory_space=pltpu.VMEM),
        compiler_params=pltpu.CompilerParams(vmem_limit_bytes=VMEM_BYTES - 4 * gate_w.size - E1 * MIB // 4),
        name="enter",
    )(gate_w, up_w)


def gather_kernel(halves, *refs):
    chunks, outs = refs[:-halves], refs[-halves:]
    for out, half in zip(outs, range(halves)):
        width = out.shape[2]
        for i, ref in enumerate(chunks):
            out[i] = ref[:, half * width:(half + 1) * width]


def gather_rows(chunks, halves):
    rows, model = chunks[0].shape
    vmem = pl.BlockSpec(memory_space=pltpu.VMEM)
    return pl.pallas_call(
        functools.partial(gather_kernel, halves),
        out_shape=[jax.ShapeDtypeStruct((len(chunks), rows, model // halves), chunks[0].dtype)] * halves,
        in_specs=[vmem] * len(chunks),
        out_specs=[vmem] * halves,
        compiler_params=pltpu.CompilerParams(vmem_limit_bytes=2 * MIB),
    )(*chunks)


def pieces(refs):
    return [ref.at[i] for ref in refs for i in range(ref.shape[0])]


def project(refs, half, depth, gate_ref, up_ref, gate_sum, up_sum):
    span_of = gate_ref.shape[0] // HALVES
    starts = [half * span_of if ref.shape[2] > span_of else 0 for ref in refs for _ in range(ref.shape[0])]
    chunks = list(zip(pieces(refs), starts))

    def step(i, carry):
        at = pl.multiple_of(i * depth, depth)
        tokens = [c[:, pl.ds(pl.multiple_of(first + at, 128), depth)].astype(jnp.float32) for c, first in chunks]
        tokens = jnp.concatenate(tokens, axis=0).astype(jnp.bfloat16)
        span = pl.ds(pl.multiple_of(half * span_of + at, 128), depth)
        gate_sum[...] += jnp.dot(tokens, gate_ref[span, :], preferred_element_type=jnp.float32)
        up_sum[...] += jnp.dot(tokens, up_ref[span, :], preferred_element_type=jnp.float32)
        return carry

    lax.fori_loop(0, span_of // depth, step, 0)


def first_kernel(n_in, depth, *refs):
    gate_ref, up_ref, down_ref, gate_sum, up_sum, down_low, semaphore = refs[n_in:]
    fetch = pltpu.make_async_copy(down_ref.at[:, pl.ds(0, down_low.shape[1])], down_low, semaphore)
    fetch.start()
    gate_sum[...] = jnp.zeros_like(gate_sum)
    up_sum[...] = jnp.zeros_like(up_sum)
    project(refs[:n_in], 0, depth, gate_ref, up_ref, gate_sum, up_sum)
    fetch.wait()


def second_kernel(n_in, n_out, depth, width, *refs):
    gate_ref, up_ref, down_ref, gate_first, up_first, down_low, _ = refs[n_in:n_in + 7]
    outs = pieces(refs[n_in + 7:n_in + 7 + n_out])
    gate_sum, up_sum, hidden, down_high, semaphores = refs[n_in + 7 + n_out:]
    low = down_low.shape[1]
    count = down_high.shape[1] // width

    def fetch(i):
        source = down_ref.at[:, pl.ds(low + i * width, width)]
        return pltpu.make_async_copy(source, down_high.at[:, pl.ds(i * width, width)], semaphores.at[i])

    for i in range(count):
        fetch(i).start()
    gate_sum[...] = gate_first[...]
    up_sum[...] = up_first[...]
    project(refs[:n_in], 1, depth, gate_ref, up_ref, gate_sum, up_sum)
    gate = gate_sum[...]
    hidden[...] = (gate / (1.0 + jnp.exp(-gate)) * up_sum[...]).astype(jnp.bfloat16)
    rows = outs[0].shape[0]

    def expand(source, at, base):
        partial = jnp.dot(hidden[...], source[:, pl.ds(at, width)], preferred_element_type=jnp.float32)
        for j, out in enumerate(outs):
            out[:, pl.ds(base + at, width)] = partial[j * rows:(j + 1) * rows].astype(jnp.bfloat16)

    for i in range(low // width):
        expand(down_low, i * width, 0)
    for i in range(count):
        fetch(i).wait()
        expand(down_high, i * width, low)


def block_of(model, most):
    return max(b for b in range(128, most + 1, 128) if model % b == 0)


def expert(first_blocks, second_blocks, out_counts, gate_w, up_w, down_w, entered):
    rows = first_blocks[0].shape[1]
    model, units = gate_w.shape
    half = model // HALVES
    low = model // LOW
    depth, width = block_of(half, DEPTH), block_of(low, WIDTH)
    total = rows * sum(b.shape[0] for b in first_blocks)
    sums = jax.ShapeDtypeStruct((total, units), jnp.float32)
    vmem, hbm = pl.BlockSpec(memory_space=pltpu.VMEM), pl.BlockSpec(memory_space=pl.ANY)
    room = VMEM_BYTES - 4 * gate_w.size
    cost = pl.CostEstimate(
        flops=3 * total * model * units,
        bytes_accessed=3 * model * units + 2 * total * model,
        transcendentals=total * units,
    )
    gate_sum, up_sum, down_low = pl.pallas_call(
        functools.partial(first_kernel, len(first_blocks), depth),
        out_shape=[sums, sums, jax.ShapeDtypeStruct((units, low), down_w.dtype)],
        in_specs=[vmem] * (len(first_blocks) + 2) + [hbm],
        out_specs=[vmem] * 3,
        scratch_shapes=[pltpu.SemaphoreType.DMA],
        compiler_params=pltpu.CompilerParams(vmem_limit_bytes=room - L1 * MIB),
        cost_estimate=cost,
        name="ffn_first",
    )(*first_blocks, gate_w, up_w, down_w)
    return pl.pallas_call(
        functools.partial(second_kernel, len(second_blocks), len(out_counts), depth, width),
        out_shape=[jax.ShapeDtypeStruct((n, rows, model), jnp.bfloat16) for n in out_counts],
        in_specs=[vmem] * (len(second_blocks) + 2) + [hbm] + [vmem] * 3 + [hbm],
        out_specs=[vmem] * len(out_counts),
        scratch_shapes=[
            pltpu.VMEM((total, units), jnp.float32),
            pltpu.VMEM((total, units), jnp.float32),
            pltpu.VMEM((total, units), jnp.bfloat16),
            pltpu.VMEM((units, model - low), down_w.dtype),
            pltpu.SemaphoreType.DMA((model // width,)),
        ],
        compiler_params=pltpu.CompilerParams(vmem_limit_bytes=room - L2 * MIB),
        cost_estimate=cost,
        name="ffn",
    )(*second_blocks, gate_w, up_w, down_w, gate_sum, up_sum, down_low, entered)


HALVES = 2
LOW = 4
L1 = 15
L2 = 16
E1 = 3
XOR = True
DEPTH = 1792
WIDTH = 1792


def combine_kernel(ids_ref, gate_ref, *refs):
    terms, out = refs[:-1], refs[-1]
    me = lax.axis_index("ep")
    ids = ids_ref[...]
    scores = gate_ref[...].astype(jnp.float32)
    weights = 2.5 * scores / jnp.sum(scores, axis=1, keepdims=True)
    total = jnp.zeros(out.shape, jnp.float32)
    for k, term in enumerate(terms):
        label = me ^ k if mirrors(len(terms)) else lax.rem(me + k, len(terms))
        weight = jnp.sum(jnp.where(ids == label, weights, 0.0), axis=1, keepdims=True)
        total = total + weight * term[0].astype(jnp.float32)
    out[...] = total.astype(jnp.bfloat16)


def combine(expert_ids, gate_fixed, terms):
    vmem = pl.BlockSpec(memory_space=pltpu.VMEM)
    return pl.pallas_call(
        combine_kernel,
        out_shape=jax.ShapeDtypeStruct(terms[0].shape[1:], jnp.bfloat16),
        in_specs=[vmem] * (len(terms) + 2),
        out_specs=vmem,
        compiler_params=pltpu.CompilerParams(vmem_limit_bytes=8 * MIB),
        name="combine",
    )(expert_ids, gate_fixed, *terms)


def sum_kernel(spans, *refs):
    out = refs[-1]
    for i in range(out.shape[0]):
        total = refs[0][spans[0] + i].astype(jnp.float32)
        for ref, first in zip(refs[1:-1], spans[1:]):
            total = total + ref[first + i].astype(jnp.float32)
        out[i] = total.astype(out.dtype)


def add(count, *terms):
    vmem = pl.BlockSpec(memory_space=pltpu.VMEM)
    arrays = [array for array, _ in terms]
    rows, model = arrays[0].shape[1:]
    return pl.pallas_call(
        functools.partial(sum_kernel, [first for _, first in terms]),
        out_shape=jax.ShapeDtypeStruct((count, rows, model), arrays[0].dtype),
        in_specs=[vmem] * len(arrays),
        out_specs=vmem,
        compiler_params=pltpu.CompilerParams(vmem_limit_bytes=4 * MIB),
    )(*arrays)


def per_device(tokens, expert_ids, gate_fixed, w_gate, w_up, w_down):
    n_ep = lax.axis_size("ep")
    n_x = lax.axis_size("tok") // CORES
    entered = enter(w_gate[0], w_up[0])
    arrived = [shift(tokens, "ep", k) for k in range(1, n_ep)]
    lines = [tokens] + [shift(tokens, "tok", j, CORES) for j in range(1, n_x)]
    stage = gather_rows([tokens], 1)[0]
    arrived = gather_rows(arrived, HALVES)
    whole = [stage] + [lines[j][None] for j in range(1, n_x)]
    whole += [core_swap(w) for w in whole]
    parted = []
    for half in range(HALVES):
        blocks = [arrived[half]]
        blocks += [shift(arrived[half], "tok", j, CORES) for j in range(1, n_x)]
        blocks += [core_swap(b) for b in blocks]
        parted.append([b for pair in zip(whole, blocks) for b in pair])
    sizes = [n_ep] + [n_ep - 1, 1] * (n_x - 1)
    parts = expert(*parted, sizes * CORES, w_gate[0], w_up[0], w_down[0], entered)
    mine, theirs = parts[:len(sizes)], parts[len(sizes):]
    far = [[] for _ in range(n_ep)]
    spans = ((0, n_ep - 1, 1), (1, n_ep - 2, 1), (2, 0, n_ep - 2))
    for j in range(1, n_x):
        last, rest = 2 * j, 2 * j - 1
        tail = core_swap(theirs[last])
        body = core_swap(theirs[rest])
        for part, first, count in spans:
            pair = ((mine[last], 0), (tail, 0)) if part == 0 else ((mine[rest], first), (body, first))
            value = shift(add(count, *pair), "tok", -j, CORES)
            for k in range(count):
                far[first + k].append((value, k))
    near = core_swap(theirs[0])
    terms = []
    for k in range(n_ep):
        total = add(1, (mine[0], k), (near, k), *far[k])
        terms.append(shift(total, "ep", -k) if k else total)
    return combine(expert_ids, gate_fixed, terms)


def solution(mesh):
    in_specs = (
        P(("groups", "ep", "tok"), None),
        P(("groups", "ep", "tok"), None),
        P(("groups", "ep", "tok"), None),
        P("ep", None, "tok"),
        P("ep", None, "tok"),
        P("ep", "tok", None),
    )
    out_specs = P(("groups", "ep", "tok"), None)
    return jax.shard_map(
        per_device, mesh=mesh, in_specs=in_specs, out_specs=out_specs, check_vma=False
    )
```

```python
import functools

import jax
import jax.numpy as jnp
from jax import lax
from jax.experimental import pallas as pl
from jax.experimental.pallas import tpu as pltpu
from jax.sharding import PartitionSpec as P


CORES = 2
MIB = 1 << 20
VMEM_BYTES = 62 * MIB


def mirrors(size):
    return XOR and size & (size - 1) == 0


def shift(value, axis, amount, stride=1):
    size = lax.axis_size(axis) // stride
    target = (lambda i: i ^ abs(amount)) if mirrors(size) else (lambda i: (i + amount) % size)
    pairs = [(i * stride + r, target(i) * stride + r) for i in range(size) for r in range(stride)]
    return lax.ppermute(value, axis, pairs)


def core_swap(value):
    size = lax.axis_size("tok")
    return lax.ppermute(value, "tok", [(i, i ^ 1) for i in range(size)])


def enter_kernel(gate_ref, up_ref, out_ref):
    out_ref[...] = jnp.zeros_like(out_ref)


def enter(gate_w, up_w):
    hbm = pl.BlockSpec(memory_space=pl.ANY)
    return pl.pallas_call(
        enter_kernel,
        out_shape=jax.ShapeDtypeStruct((8, 128), jnp.float32),
        in_specs=[hbm, hbm],
        out_specs=pl.BlockSpec(memory_space=pltpu.VMEM),
        compiler_params=pltpu.CompilerParams(vmem_limit_bytes=VMEM_BYTES - 4 * gate_w.size - E1 * MIB // 4),
        name="enter",
    )(gate_w, up_w)


def gather_kernel(halves, *refs):
    chunks, outs = refs[:-halves], refs[-halves:]
    for out, half in zip(outs, range(halves)):
        width = out.shape[2]
        for i, ref in enumerate(chunks):
            out[i] = ref[:, half * width:(half + 1) * width]


def gather_rows(chunks, halves):
    rows, model = chunks[0].shape
    vmem = pl.BlockSpec(memory_space=pltpu.VMEM)
    return pl.pallas_call(
        functools.partial(gather_kernel, halves),
        out_shape=[jax.ShapeDtypeStruct((len(chunks), rows, model // halves), chunks[0].dtype)] * halves,
        in_specs=[vmem] * len(chunks),
        out_specs=[vmem] * halves,
        compiler_params=pltpu.CompilerParams(vmem_limit_bytes=2 * MIB),
    )(*chunks)


def pieces(refs):
    return [ref.at[i] for ref in refs for i in range(ref.shape[0])]


def project(refs, half, depth, gate_ref, up_ref, gate_sum, up_sum):
    span_of = gate_ref.shape[0] // HALVES
    starts = [half * span_of if ref.shape[2] > span_of else 0 for ref in refs for _ in range(ref.shape[0])]
    chunks = list(zip(pieces(refs), starts))

    def step(i, carry):
        at = pl.multiple_of(i * depth, depth)
        tokens = [c[:, pl.ds(pl.multiple_of(first + at, 128), depth)].astype(jnp.float32) for c, first in chunks]
        tokens = jnp.concatenate(tokens, axis=0).astype(jnp.bfloat16)
        span = pl.ds(pl.multiple_of(half * span_of + at, 128), depth)
        gate_sum[...] += jnp.dot(tokens, gate_ref[span, :], preferred_element_type=jnp.float32)
        up_sum[...] += jnp.dot(tokens, up_ref[span, :], preferred_element_type=jnp.float32)
        return carry

    lax.fori_loop(0, span_of // depth, step, 0)


def first_kernel(n_in, depth, *refs):
    gate_ref, up_ref, down_ref, gate_sum, up_sum, down_low, semaphore = refs[n_in:]
    fetch = pltpu.make_async_copy(down_ref.at[:, pl.ds(0, down_low.shape[1])], down_low, semaphore)
    fetch.start()
    gate_sum[...] = jnp.zeros_like(gate_sum)
    up_sum[...] = jnp.zeros_like(up_sum)
    project(refs[:n_in], 0, depth, gate_ref, up_ref, gate_sum, up_sum)
    fetch.wait()


def second_kernel(n_in, n_out, depth, width, *refs):
    gate_ref, up_ref, down_ref, gate_first, up_first, down_low, _ = refs[n_in:n_in + 7]
    outs = pieces(refs[n_in + 7:n_in + 7 + n_out])
    gate_sum, up_sum, hidden, down_high, semaphores = refs[n_in + 7 + n_out:]
    low = down_low.shape[1]
    count = down_high.shape[1] // width

    def fetch(i):
        source = down_ref.at[:, pl.ds(low + i * width, width)]
        return pltpu.make_async_copy(source, down_high.at[:, pl.ds(i * width, width)], semaphores.at[i])

    for i in range(count):
        fetch(i).start()
    gate_sum[...] = gate_first[...]
    up_sum[...] = up_first[...]
    project(refs[:n_in], 1, depth, gate_ref, up_ref, gate_sum, up_sum)
    gate = gate_sum[...]
    hidden[...] = (gate / (1.0 + jnp.exp(-gate)) * up_sum[...]).astype(jnp.bfloat16)
    rows = outs[0].shape[0]

    def expand(source, at, base):
        partial = jnp.dot(hidden[...], source[:, pl.ds(at, width)], preferred_element_type=jnp.float32)
        for j, out in enumerate(outs):
            out[:, pl.ds(base + at, width)] = partial[j * rows:(j + 1) * rows].astype(jnp.bfloat16)

    for i in range(low // width):
        expand(down_low, i * width, 0)
    for i in range(count):
        fetch(i).wait()
        expand(down_high, i * width, low)


def block_of(model, most):
    return max(b for b in range(128, most + 1, 128) if model % b == 0)


def expert(first_blocks, second_blocks, out_counts, gate_w, up_w, down_w, entered):
    rows = first_blocks[0].shape[1]
    model, units = gate_w.shape
    half = model // HALVES
    low = model // LOW
    depth, width = block_of(half, DEPTH), block_of(low, WIDTH)
    total = rows * sum(b.shape[0] for b in first_blocks)
    sums = jax.ShapeDtypeStruct((total, units), jnp.float32)
    vmem, hbm = pl.BlockSpec(memory_space=pltpu.VMEM), pl.BlockSpec(memory_space=pl.ANY)
    room = VMEM_BYTES - 4 * gate_w.size
    cost = pl.CostEstimate(
        flops=3 * total * model * units,
        bytes_accessed=3 * model * units + 2 * total * model,
        transcendentals=total * units,
    )
    gate_sum, up_sum, down_low = pl.pallas_call(
        functools.partial(first_kernel, len(first_blocks), depth),
        out_shape=[sums, sums, jax.ShapeDtypeStruct((units, low), down_w.dtype)],
        in_specs=[vmem] * (len(first_blocks) + 2) + [hbm],
        out_specs=[vmem] * 3,
        scratch_shapes=[pltpu.SemaphoreType.DMA],
        compiler_params=pltpu.CompilerParams(vmem_limit_bytes=room - L1 * MIB),
        cost_estimate=cost,
        name="ffn_first",
    )(*first_blocks, gate_w, up_w, down_w)
    return pl.pallas_call(
        functools.partial(second_kernel, len(second_blocks), len(out_counts), depth, width),
        out_shape=[jax.ShapeDtypeStruct((n, rows, model), jnp.bfloat16) for n in out_counts],
        in_specs=[vmem] * (len(second_blocks) + 2) + [hbm] + [vmem] * 3 + [hbm],
        out_specs=[vmem] * len(out_counts),
        scratch_shapes=[
            pltpu.VMEM((total, units), jnp.float32),
            pltpu.VMEM((total, units), jnp.float32),
            pltpu.VMEM((total, units), jnp.bfloat16),
            pltpu.VMEM((units, model - low), down_w.dtype),
            pltpu.SemaphoreType.DMA((model // width,)),
        ],
        compiler_params=pltpu.CompilerParams(vmem_limit_bytes=room - L2 * MIB),
        cost_estimate=cost,
        name="ffn",
    )(*second_blocks, gate_w, up_w, down_w, gate_sum, up_sum, down_low, entered)


HALVES = 2
LOW = 4
L1 = 15
L2 = 16
E1 = 3
XOR = False
DEPTH = 1792
WIDTH = 1792


def combine_kernel(ids_ref, gate_ref, *refs):
    terms, out = refs[:-1], refs[-1]
    me = lax.axis_index("ep")
    ids = ids_ref[...]
    scores = gate_ref[...].astype(jnp.float32)
    weights = 2.5 * scores / jnp.sum(scores, axis=1, keepdims=True)
    total = jnp.zeros(out.shape, jnp.float32)
    for k, term in enumerate(terms):
        label = me ^ k if mirrors(len(terms)) else lax.rem(me + k, len(terms))
        weight = jnp.sum(jnp.where(ids == label, weights, 0.0), axis=1, keepdims=True)
        total = total + weight * term[0].astype(jnp.float32)
    out[...] = total.astype(jnp.bfloat16)


def combine(expert_ids, gate_fixed, terms):
    vmem = pl.BlockSpec(memory_space=pltpu.VMEM)
    return pl.pallas_call(
        combine_kernel,
        out_shape=jax.ShapeDtypeStruct(terms[0].shape[1:], jnp.bfloat16),
        in_specs=[vmem] * (len(terms) + 2),
        out_specs=vmem,
        compiler_params=pltpu.CompilerParams(vmem_limit_bytes=8 * MIB),
        name="combine",
    )(expert_ids, gate_fixed, *terms)


def sum_kernel(spans, *refs):
    out = refs[-1]
    for i in range(out.shape[0]):
        total = refs[0][spans[0] + i].astype(jnp.float32)
        for ref, first in zip(refs[1:-1], spans[1:]):
            total = total + ref[first + i].astype(jnp.float32)
        out[i] = total.astype(out.dtype)


def add(count, *terms):
    vmem = pl.BlockSpec(memory_space=pltpu.VMEM)
    arrays = [array for array, _ in terms]
    rows, model = arrays[0].shape[1:]
    return pl.pallas_call(
        functools.partial(sum_kernel, [first for _, first in terms]),
        out_shape=jax.ShapeDtypeStruct((count, rows, model), arrays[0].dtype),
        in_specs=[vmem] * len(arrays),
        out_specs=vmem,
        compiler_params=pltpu.CompilerParams(vmem_limit_bytes=4 * MIB),
    )(*arrays)


def per_device(tokens, expert_ids, gate_fixed, w_gate, w_up, w_down):
    n_ep = lax.axis_size("ep")
    n_x = lax.axis_size("tok") // CORES
    entered = enter(w_gate[0], w_up[0])
    arrived = [shift(tokens, "ep", k) for k in range(1, n_ep)]
    stage = gather_rows([gather_rows([tokens], 1)[0][0], arrived[0]], 1)[0]
    arrived = gather_rows(arrived[1:], HALVES)
    whole = [stage] + [shift(stage, "tok", j, CORES) for j in range(1, n_x)]
    whole += [core_swap(w) for w in whole]
    parted = []
    for half in range(HALVES):
        blocks = [arrived[half]]
        blocks += [shift(arrived[half], "tok", j, CORES) for j in range(1, n_x)]
        blocks += [core_swap(b) for b in blocks]
        parted.append([b for pair in zip(whole, blocks) for b in pair])
    sizes = [n_ep] + [n_ep - 1, 1] * (n_x - 1)
    parts = expert(*parted, sizes * CORES, w_gate[0], w_up[0], w_down[0], entered)
    mine, theirs = parts[:len(sizes)], parts[len(sizes):]
    far = [[] for _ in range(n_ep)]
    spans = ((0, n_ep - 1, 1), (1, n_ep - 2, 1), (2, 0, n_ep - 2))
    for j in range(1, n_x):
        last, rest = 2 * j, 2 * j - 1
        tail = core_swap(theirs[last])
        body = core_swap(theirs[rest])
        for part, first, count in spans:
            pair = ((mine[last], 0), (tail, 0)) if part == 0 else ((mine[rest], first), (body, first))
            value = shift(add(count, *pair), "tok", -j, CORES)
            for k in range(count):
                far[first + k].append((value, k))
    near = core_swap(theirs[0])
    terms = []
    for k in range(n_ep):
        total = add(1, (mine[0], k), (near, k), *far[k])
        terms.append(shift(total, "ep", -k) if k else total)
    return combine(expert_ids, gate_fixed, terms)


def solution(mesh):
    in_specs = (
        P(("groups", "ep", "tok"), None),
        P(("groups", "ep", "tok"), None),
        P(("groups", "ep", "tok"), None),
        P("ep", None, "tok"),
        P("ep", None, "tok"),
        P("ep", "tok", None),
    )
    out_specs = P(("groups", "ep", "tok"), None)
    return jax.shard_map(
        per_device, mesh=mesh, in_specs=in_specs, out_specs=out_specs, check_vma=False
    )
```

```python
import functools

import jax
import jax.numpy as jnp
from jax import lax
from jax.experimental import pallas as pl
from jax.experimental.pallas import tpu as pltpu
from jax.sharding import PartitionSpec as P


CORES = 2
PARTS = 1
MIB = 1 << 20
VMEM_BYTES = 62 * MIB


def mirrors(size):
    return XOR and size & (size - 1) == 0


def shift(value, axis, amount, stride=1):
    size = lax.axis_size(axis) // stride
    target = (lambda i: i ^ abs(amount)) if mirrors(size) else (lambda i: (i + amount) % size)
    pairs = [(i * stride + r, target(i) * stride + r) for i in range(size) for r in range(stride)]
    return lax.ppermute(value, axis, pairs)


def core_swap(value):
    size = lax.axis_size("tok")
    return lax.ppermute(value, "tok", [(i, i ^ 1) for i in range(size)])


def enter_kernel(gate_ref, up_ref, out_ref):
    out_ref[...] = jnp.zeros_like(out_ref)


def enter(gate_w, up_w):
    hbm = pl.BlockSpec(memory_space=pl.ANY)
    return pl.pallas_call(
        enter_kernel,
        out_shape=jax.ShapeDtypeStruct((8, 128), jnp.float32),
        in_specs=[hbm, hbm],
        out_specs=pl.BlockSpec(memory_space=pltpu.VMEM),
        compiler_params=pltpu.CompilerParams(vmem_limit_bytes=VMEM_BYTES - 4 * gate_w.size - E1 * MIB // 4),
        name="enter",
    )(gate_w, up_w)


def gather_kernel(halves, *refs):
    chunks, outs = refs[:-halves], refs[-halves:]
    for out, half in zip(outs, range(halves)):
        width = out.shape[2]
        for i, ref in enumerate(chunks):
            out[i] = ref[:, half * width:(half + 1) * width]


def gather_rows(chunks, halves):
    rows, model = chunks[0].shape
    vmem = pl.BlockSpec(memory_space=pltpu.VMEM)
    return pl.pallas_call(
        functools.partial(gather_kernel, halves),
        out_shape=[jax.ShapeDtypeStruct((len(chunks), rows, model // halves), chunks[0].dtype)] * halves,
        in_specs=[vmem] * len(chunks),
        out_specs=[vmem] * halves,
        compiler_params=pltpu.CompilerParams(vmem_limit_bytes=2 * MIB),
    )(*chunks)


def pieces(refs):
    return [ref.at[i] for ref in refs for i in range(ref.shape[0])]


def project(refs, half, depth, gate_ref, up_ref, gate_sum, up_sum):
    span_of = gate_ref.shape[0] // HALVES
    starts = [half * span_of if ref.shape[2] > span_of else 0 for ref in refs for _ in range(ref.shape[0])]
    chunks = list(zip(pieces(refs), starts))

    def step(i, carry):
        at = pl.multiple_of(i * depth, depth)
        tokens = [c[:, pl.ds(pl.multiple_of(first + at, 128), depth)].astype(jnp.float32) for c, first in chunks]
        tokens = jnp.concatenate(tokens, axis=0).astype(jnp.bfloat16)
        span = pl.ds(pl.multiple_of(half * span_of + at, 128), depth)
        gate_sum[...] += jnp.dot(tokens, gate_ref[span, :], preferred_element_type=jnp.float32)
        up_sum[...] += jnp.dot(tokens, up_ref[span, :], preferred_element_type=jnp.float32)
        return carry

    lax.fori_loop(0, span_of // depth, step, 0)


def first_kernel(n_in, depth, *refs):
    gate_ref, up_ref, down_ref, gate_sum, up_sum, down_low, semaphore = refs[n_in:]
    fetch = pltpu.make_async_copy(down_ref.at[:, pl.ds(0, down_low.shape[1])], down_low, semaphore)
    fetch.start()
    gate_sum[...] = jnp.zeros_like(gate_sum)
    up_sum[...] = jnp.zeros_like(up_sum)
    project(refs[:n_in], 0, depth, gate_ref, up_ref, gate_sum, up_sum)
    fetch.wait()


def second_kernel(n_in, n_out, depth, width, *refs):
    gate_ref, up_ref, down_ref, gate_first, up_first, down_low, _ = refs[n_in:n_in + 7]
    outs = pieces(refs[n_in + 7:n_in + 7 + n_out])
    gate_sum, up_sum, hidden, down_high, semaphores = refs[n_in + 7 + n_out:]
    low = down_low.shape[1]
    count = down_high.shape[1] // width

    def fetch(i):
        source = down_ref.at[:, pl.ds(low + i * width, width)]
        return pltpu.make_async_copy(source, down_high.at[:, pl.ds(i * width, width)], semaphores.at[i])

    for i in range(count):
        fetch(i).start()
    gate_sum[...] = gate_first[...]
    up_sum[...] = up_first[...]
    project(refs[:n_in], 1, depth, gate_ref, up_ref, gate_sum, up_sum)
    gate = gate_sum[...]
    hidden[...] = (gate / (1.0 + jnp.exp(-gate)) * up_sum[...]).astype(jnp.bfloat16)
    rows = outs[0].shape[0]

    def expand(source, at, base):
        partial = jnp.dot(hidden[...], source[:, pl.ds(at, width)], preferred_element_type=jnp.float32)
        for j, out in enumerate(outs):
            out[:, pl.ds(base + at, width)] = partial[j * rows:(j + 1) * rows].astype(jnp.bfloat16)

    for i in range(low // width):
        expand(down_low, i * width, 0)
    for i in range(count):
        fetch(i).wait()
        expand(down_high, i * width, low)


def block_of(model, most):
    return max(b for b in range(128, most + 1, 128) if model % b == 0)


def expert(first_blocks, second_blocks, out_counts, gate_w, up_w, down_w, entered):
    rows = first_blocks[0].shape[1]
    model, units = gate_w.shape
    half = model // HALVES
    low = model // LOW
    depth, width = block_of(half, DEPTH), block_of(low, WIDTH)
    total = rows * sum(b.shape[0] for b in first_blocks)
    sums = jax.ShapeDtypeStruct((total, units), jnp.float32)
    vmem, hbm = pl.BlockSpec(memory_space=pltpu.VMEM), pl.BlockSpec(memory_space=pl.ANY)
    room = VMEM_BYTES - 4 * gate_w.size
    cost = pl.CostEstimate(
        flops=3 * total * model * units,
        bytes_accessed=3 * model * units + 2 * total * model,
        transcendentals=total * units,
    )
    gate_sum, up_sum, down_low = pl.pallas_call(
        functools.partial(first_kernel, len(first_blocks), depth),
        out_shape=[sums, sums, jax.ShapeDtypeStruct((units, low), down_w.dtype)],
        in_specs=[vmem] * (len(first_blocks) + 2) + [hbm],
        out_specs=[vmem] * 3,
        scratch_shapes=[pltpu.SemaphoreType.DMA],
        compiler_params=pltpu.CompilerParams(vmem_limit_bytes=room - L1 * MIB),
        cost_estimate=cost,
        name="ffn_first",
    )(*first_blocks, gate_w, up_w, down_w)
    return pl.pallas_call(
        functools.partial(second_kernel, len(second_blocks), len(out_counts), depth, width),
        out_shape=[jax.ShapeDtypeStruct((n, rows, model), jnp.bfloat16) for n in out_counts],
        in_specs=[vmem] * (len(second_blocks) + 2) + [hbm] + [vmem] * 3 + [hbm],
        out_specs=[vmem] * len(out_counts),
        scratch_shapes=[
            pltpu.VMEM((total, units), jnp.float32),
            pltpu.VMEM((total, units), jnp.float32),
            pltpu.VMEM((total, units), jnp.bfloat16),
            pltpu.VMEM((units, model - low), down_w.dtype),
            pltpu.SemaphoreType.DMA((model // width,)),
        ],
        compiler_params=pltpu.CompilerParams(vmem_limit_bytes=room - L2 * MIB),
        cost_estimate=cost,
        name="ffn",
    )(*second_blocks, gate_w, up_w, down_w, gate_sum, up_sum, down_low, entered)


HALVES = 2
LOW = 4
L1 = 15
L2 = 16
E1 = 3
XOR = False
DEPTH = 1792
WIDTH = 1792


def gating_kernel(ids_ref, gate_ref, out):
    me = lax.axis_index("ep")
    ids = ids_ref[...]
    scores = gate_ref[...].astype(jnp.float32)
    weights = 2.5 * scores / jnp.sum(scores, axis=1, keepdims=True)
    for k in range(out.shape[0]):
        label = me ^ k if mirrors(out.shape[0]) else lax.rem(me + k, out.shape[0])
        weight = jnp.sum(jnp.where(ids == label, weights, 0.0), axis=1, keepdims=True)
        out[k] = jnp.broadcast_to(weight, out.shape[1:])


def gating(expert_ids, gate_fixed, n_ep):
    vmem = pl.BlockSpec(memory_space=pltpu.VMEM)
    return pl.pallas_call(
        gating_kernel,
        out_shape=jax.ShapeDtypeStruct((n_ep, expert_ids.shape[0], 128), jnp.float32),
        in_specs=[vmem, vmem],
        out_specs=vmem,
        compiler_params=pltpu.CompilerParams(vmem_limit_bytes=2 * MIB),
        name="gating",
    )(expert_ids, gate_fixed)


def combine_kernel(parts, weights_ref, *refs):
    terms, out, buffer, semaphores = refs[:-3], refs[-3], refs[-2], refs[-1]
    width = out.shape[1] // parts
    copies = []
    for i in range(parts):
        at = slice(i * width, (i + 1) * width)
        total = jnp.zeros((out.shape[0], width), jnp.float32)
        for k, term in enumerate(terms):
            total = total + weights_ref[k][:, :1] * term[0, :, at].astype(jnp.float32)
        buffer[:, at] = total.astype(jnp.bfloat16)
        copies.append(pltpu.make_async_copy(buffer.at[:, at], out.at[:, at], semaphores.at[i]))
        copies[-1].start()
    for copy in copies:
        copy.wait()


def combine(weights, terms, parts=PARTS):
    shape = terms[0].shape[1:]
    vmem = pl.BlockSpec(memory_space=pltpu.VMEM)
    return pl.pallas_call(
        functools.partial(combine_kernel, parts),
        out_shape=jax.ShapeDtypeStruct(shape, jnp.bfloat16),
        in_specs=[vmem] * (len(terms) + 1),
        out_specs=pl.BlockSpec(memory_space=pl.ANY),
        scratch_shapes=[pltpu.VMEM(shape, jnp.bfloat16), pltpu.SemaphoreType.DMA((parts,))],
        compiler_params=pltpu.CompilerParams(vmem_limit_bytes=4 * MIB),
        name="combine",
    )(weights, *terms)


def sum_kernel(spans, *refs):
    out = refs[-1]
    for i in range(out.shape[0]):
        total = refs[0][spans[0] + i].astype(jnp.float32)
        for ref, first in zip(refs[1:-1], spans[1:]):
            total = total + ref[first + i].astype(jnp.float32)
        out[i] = total.astype(out.dtype)


def add(count, *terms):
    vmem = pl.BlockSpec(memory_space=pltpu.VMEM)
    arrays = [array for array, _ in terms]
    rows, model = arrays[0].shape[1:]
    return pl.pallas_call(
        functools.partial(sum_kernel, [first for _, first in terms]),
        out_shape=jax.ShapeDtypeStruct((count, rows, model), arrays[0].dtype),
        in_specs=[vmem] * len(arrays),
        out_specs=vmem,
        compiler_params=pltpu.CompilerParams(vmem_limit_bytes=4 * MIB),
    )(*arrays)


def per_device(tokens, expert_ids, gate_fixed, w_gate, w_up, w_down):
    n_ep = lax.axis_size("ep")
    n_x = lax.axis_size("tok") // CORES
    entered = enter(w_gate[0], w_up[0])
    arrived = [shift(tokens, "ep", k) for k in range(1, n_ep)]
    stage = gather_rows([gather_rows([tokens], 1)[0][0], arrived[0]], 1)[0]
    arrived = gather_rows(arrived[1:], HALVES)
    whole = [stage] + [shift(stage, "tok", j, CORES) for j in range(1, n_x)]
    whole += [core_swap(w) for w in whole]
    parted = []
    for half in range(HALVES):
        blocks = [arrived[half]]
        blocks += [shift(arrived[half], "tok", j, CORES) for j in range(1, n_x)]
        blocks += [core_swap(b) for b in blocks]
        parted.append([b for pair in zip(whole, blocks) for b in pair])
    sizes = [n_ep] + [n_ep - 1, 1] * (n_x - 1)
    parts = expert(*parted, sizes * CORES, w_gate[0], w_up[0], w_down[0], entered)
    mine, theirs = parts[:len(sizes)], parts[len(sizes):]
    far = [[] for _ in range(n_ep)]
    spans = ((0, n_ep - 1, 1), (1, n_ep - 2, 1), (2, 0, n_ep - 2))
    for j in range(1, n_x):
        last, rest = 2 * j, 2 * j - 1
        tail = core_swap(theirs[last])
        body = core_swap(theirs[rest])
        for part, first, count in spans:
            pair = ((mine[last], 0), (tail, 0)) if part == 0 else ((mine[rest], first), (body, first))
            value = shift(add(count, *pair), "tok", -j, CORES)
            for k in range(count):
                far[first + k].append((value, k))
    near = core_swap(theirs[0])
    terms = []
    for k in range(n_ep):
        total = add(1, (mine[0], k), (near, k), *far[k])
        terms.append(shift(total, "ep", -k) if k else total)
    return combine(gating(expert_ids, gate_fixed, n_ep), terms)


def solution(mesh):
    in_specs = (
        P(("groups", "ep", "tok"), None),
        P(("groups", "ep", "tok"), None),
        P(("groups", "ep", "tok"), None),
        P("ep", None, "tok"),
        P("ep", None, "tok"),
        P("ep", "tok", None),
    )
    out_specs = P(("groups", "ep", "tok"), None)
    return jax.shard_map(
        per_device, mesh=mesh, in_specs=in_specs, out_specs=out_specs, check_vma=False
    )
```
